32 devices in a mesh: rep: 16 (over z, y, x), shard: 2 (over core).
Axes of the slice: x: 2, y: 2, z: 4, core: 2. Of those that a mesh axis runs over, the one named last changes fastest.
Arguments:
- tokens_in: bfloat16 [8192, 768], P(('rep', 'shard')), may hold values from -6 to 6
- cotangent: bfloat16 [8192, 768], P(('rep', 'shard')), may hold values from -6 to 6
- seq_lengths: int32 [32, 4], P(('rep', 'shard')), may hold values from 1 to 128, 256 in all within a row
- live_counts: int32 [32], P(('rep', 'shard')), may hold values from 64 to 256, as said below
- ln1_gain: bfloat16 [768], P('shard'), may hold values from 0.5 to 1.5
- ln1_shift: bfloat16 [768], P('shard'), may hold values from -3 to 3
- w_qkv: bfloat16 [768, 2304], P('shard'), may hold values from -0.21875 to 0.21875
- q_bias: bfloat16 [768], P('shard'), may hold values from -3 to 3
- v_bias: bfloat16 [768], P('shard'), may hold values from -3 to 3
- w_out: bfloat16 [768, 768], P('shard'), may hold values from -0.4375 to 0.4375
- out_bias: bfloat16 [768], P('shard'), may hold values from -3 to 3
- ln2_gain: bfloat16 [768], P('shard'), may hold values from 0.5 to 1.5
- ln2_shift: bfloat16 [768], P('shard'), may hold values from -3 to 3
- w_up: bfloat16 [768, 3072], P(None, 'shard'), may hold values from -0.21875 to 0.21875
- up_bias: bfloat16 [3072], P('shard'), may hold values from -3 to 3
- w_down: bfloat16 [3072, 768], P('shard'), may hold values from -0.109375 to 0.109375
- down_bias: bfloat16 [768], P('shard'), may hold values from -3 to 3
Outputs:
- block_out: bfloat16 [8192, 768], P(('rep', 'shard'))
- grad_tokens: bfloat16 [8192, 768], P(('rep', 'shard'))
- grad_ln1_gain: float32 [768], P('shard')
- grad_ln1_shift: float32 [768], P('shard')
- grad_w_qkv: float32 [768, 2304], P('shard')
- grad_q_bias: float32 [768], P('shard')
- grad_v_bias: float32 [768], P('shard')
- grad_w_out: float32 [768, 768], P('shard')
- grad_out_bias: float32 [768], P('shard')
- grad_ln2_gain: float32 [768], P('shard')
- grad_ln2_shift: float32 [768], P('shard')
- grad_w_up: float32 [768, 3072], P(None, 'shard')
- grad_up_bias: float32 [3072], P('shard')
- grad_w_down: float32 [3072, 768], P('shard')
- grad_down_bias: float32 [768], P('shard')
The draws below stay inside these ranges and needn't reach their ends.
Inputs may be any that keep to these rules, and one draw needn't show every extreme that they name: `live_counts`: each device's live slots; some device has all 256 live in every draw. `seq_lengths`: each row sums to 256.
All inputs are finite; a program needn't handle non-finite values.
Results may differ from the reference program's by a relative error of at most 0.012.
Values may be sent and summed in bfloat16 or wider, within the bound.
No kernel may reach another device: no remote copies, remote signals or barrier semaphores. Data moves between devices by JAX's collectives and lax.ppermute only.
A program may use at most 192 MiB of HBM per device.

```python
import math
import jax
import jax.numpy as jnp
import numpy as np
from jax import lax

D = 768
HEAD_DIM = 64
FF = 3072
TOK_DEV = 256
SEQS = 4
DEVS = 32
TOKENS = 8192


def draw_live_counts(key, part):
    key_count, key_pick = jax.random.split(key)
    drawn_counts = jax.random.randint(key_count, (DEVS,), TOK_DEV // 4, TOK_DEV + 1)
    chosen = jax.random.randint(key_pick, (), 0, DEVS)
    return jnp.where(jnp.arange(DEVS) == chosen, TOK_DEV, drawn_counts).astype(jnp.int32)


def steps_of(stream_key, extent, cuts, least, high):
    loudness = 1.0
    for dim, parts in cuts:
        heights = jax.random.uniform(jax.random.fold_in(jax.random.fold_in(stream_key, 6), dim), (parts,), jnp.float32, least / len(cuts), high / len(cuts))
        loudness = loudness * jnp.repeat(jnp.exp(heights), extent[dim] // parts).reshape((-1,) + (1,) * (len(extent) - 1 - dim))
    return loudness


def split_up(number_of, total, bound, lean):
    weights = [(1 << 20) // math.isqrt(standing ** lean) + 1 for standing in range(2, number_of + 1)]
    surplus, counts = total - bound - (number_of - 1), [1] * (number_of - 1)
    while surplus > 0:
        candidates = [i for i in range(number_of - 1) if counts[i] < bound]
        whole, left = sum([weights[i] for i in candidates]), surplus
        for i in candidates:
            extra = min(bound - counts[i], max(1, left * weights[i] // whole), surplus)
            counts[i] = counts[i] + extra
            surplus = surplus - extra
    return np.array([bound] + counts)


def uneven(own_key, count, total, limit, slope):
    if count == 2:
        one = jax.random.randint(own_key, (), max(1, total - limit), min(limit, total - 1) + 1)
        return jnp.stack([one, total - one])
    sizes = jnp.asarray(split_up(count, total, limit, slope), jnp.int32)
    twos = (count - 1) // 2
    donor, receiver = sizes[1:1 + 2 * twos:2], sizes[2:2 + 2 * twos:2]
    slack = jnp.minimum(donor - 1, limit - receiver)
    passed = jax.random.randint(jax.random.fold_in(own_key, 1), (twos,), 0, 1 << 20) % (slack + 1)
    sizes = sizes.at[1:1 + 2 * twos:2].set(donor - passed).at[2:2 + 2 * twos:2].set(receiver + passed)
    return sizes[jax.random.permutation(jax.random.fold_in(own_key, 2), count)]


def scatter_about(rng, extent, spread, reach, shards=(), held_as=jnp.bfloat16):
    values = jax.random.normal(rng, extent, jnp.float32) * spread
    if len(shards) > 0:
        values = steps_of(rng, extent, shards, -0.22, 0.18) * values
    return jnp.clip(values, min=-reach, max=reach).astype(held_as)


def setup_inputs(seed: int = 0) -> dict:
    key_list = jax.random.split(jax.random.key(seed), 18)
    return {
        "tokens_in": scatter_about(key_list[0], (TOKENS, D), 1.0, 6.0, ((0, 32),)),
        "cotangent": scatter_about(key_list[1], (TOKENS, D), 1.0, 6.0, ((0, 32),)),
        "seq_lengths": jax.vmap(lambda own: uneven(own, SEQS, TOK_DEV, TOK_DEV // 2, 2))(jax.random.split(key_list[2], DEVS)).reshape((DEVS, SEQS)).astype(jnp.int32),
        "live_counts": draw_live_counts(jax.random.fold_in(key_list[17], 71), 0),
        "ln1_gain": jnp.clip(1.0 + 0.1 * jax.random.normal(key_list[4], (D,), jnp.float32), 0.5, 1.5).astype(jnp.bfloat16),
        "ln1_shift": scatter_about(key_list[5], (D,), 0.5, 3.0, ((0, 2),)),
        "w_qkv": scatter_about(key_list[6], (D, 3 * D), D ** -0.5, 0.21875, ((0, 2),)),
        "q_bias": scatter_about(key_list[7], (D,), 0.5, 3.0, ((0, 2),)),
        "v_bias": scatter_about(key_list[8], (D,), 0.5, 3.0, ((0, 2),)),
        "w_out": scatter_about(key_list[9], (D, D), (D // 4) ** -0.5, 0.4375, ((0, 2),)),
        "out_bias": scatter_about(key_list[10], (D,), 0.5, 3.0, ((0, 2),)),
        "ln2_gain": jnp.clip(1.0 + 0.1 * jax.random.normal(key_list[11], (D,), jnp.float32), 0.5, 1.5).astype(jnp.bfloat16),
        "ln2_shift": scatter_about(key_list[12], (D,), 0.5, 3.0, ((0, 2),)),
        "w_up": scatter_about(key_list[13], (D, FF), D ** -0.5, 0.21875, ((1, 2),)),
        "up_bias": scatter_about(key_list[14], (FF,), 0.5, 3.0, ((0, 2),)),
        "w_down": scatter_about(key_list[15], (FF, D), FF ** -0.5, 0.109375, ((0, 2),)),
        "down_bias": scatter_about(key_list[16], (D,), 0.5, 3.0, ((0, 2),)),
    }


epsilon_norm = 1e-05
masked_score = -1e+30

def matmul(left, right):
    return jnp.dot(left, right, preferred_element_type=jnp.float32)

def contract(form, left, right):
    return jnp.einsum(form, left.astype(jnp.float32), right.astype(jnp.float32))

def norm_forward(values, gain, shift):
    center = values - lax.optimization_barrier(jnp.mean(values, -1, keepdims=True))
    inverse = lax.rsqrt(lax.optimization_barrier(jnp.mean(center * center, -1, keepdims=True)) + epsilon_norm)
    normed = center * inverse
    return (normed * gain + shift, normed, inverse)

def norm_backward(upstream, normed, inverse, gain):
    scaled = upstream * gain
    inward = inverse * (scaled - lax.optimization_barrier(jnp.mean(scaled, -1, keepdims=True)) - normed * lax.optimization_barrier(jnp.mean(scaled * normed, -1, keepdims=True)))
    return (inward, lax.optimization_barrier(jnp.sum(upstream * normed, 0)), lax.optimization_barrier(jnp.sum(upstream, 0)))

def live_mask(length_row, live_count, row_count):
    position = jnp.arange(row_count, dtype=jnp.int32)
    bounds = jnp.cumsum(length_row.astype(jnp.int32))
    segment = lax.optimization_barrier(jnp.sum((position[:, None] >= bounds[None, :]).astype(jnp.int32), 1))
    live = position < live_count
    allowed = (segment[:, None] == segment[None, :]) & (position[None, :] <= position[:, None])
    allowed = allowed & (live[None, :] | (position[:, None] == position[None, :]))
    return (allowed, live)

def gelu_tanh(values):
    return jax.nn.gelu(values, approximate=True)

def score_block(query, keys, allowed):
    scores = contract('qhd,khd->hqk', query, keys) * query.shape[-1] ** (-0.5)
    return jnp.where(allowed[None], scores, masked_score)

def layer_pass(block_in, block_cot, length_row, live_count, forward_params, backward_params):
    gain_one, shift_one, weight_qkv, bias_query, bias_value, weight_out, bias_out, gain_two, shift_two, weight_up, bias_up, weight_down, bias_down = forward_params
    row_count = block_in.shape[0]
    width = block_in.shape[1]
    head_count = width // HEAD_DIM
    allowed, live = live_mask(length_row, live_count, row_count)
    live_col = live[:, None].astype(jnp.float32)
    tokens_f = block_in.astype(jnp.float32)
    normed_in, normed_one, inverse_one = norm_forward(tokens_f, gain_one.astype(jnp.float32), shift_one.astype(jnp.float32))
    hidden_one = normed_in.astype(jnp.bfloat16)
    bias_full = jnp.concatenate([bias_query.astype(jnp.float32), jnp.zeros((width,), jnp.float32), bias_value.astype(jnp.float32)])
    qkv = (matmul(hidden_one, weight_qkv) + bias_full).astype(jnp.bfloat16)
    query = qkv[:, :width].reshape(row_count, head_count, HEAD_DIM)
    keys = qkv[:, width:2 * width].reshape(row_count, head_count, HEAD_DIM)
    value = qkv[:, 2 * width:].reshape(row_count, head_count, HEAD_DIM)
    scores = score_block(query, keys, allowed)
    highest = lax.optimization_barrier(jnp.max(scores, -1, keepdims=True))
    logsum = highest + jnp.log(lax.optimization_barrier(jnp.sum(jnp.exp(scores - highest), -1, keepdims=True)))
    probs_b = jnp.exp(scores - logsum).astype(jnp.bfloat16)
    context = contract('hqk,khd->qhd', probs_b, value).reshape(row_count, width).astype(jnp.bfloat16)
    resid = tokens_f + matmul(context, weight_out) + bias_out.astype(jnp.float32)
    normed_mid, normed_two, inverse_two = norm_forward(resid, gain_two.astype(jnp.float32), shift_two.astype(jnp.float32))
    hidden_two = normed_mid.astype(jnp.bfloat16)
    upper = matmul(hidden_two, weight_up) + bias_up.astype(jnp.float32)
    active, gelu_pull = jax.vjp(gelu_tanh, upper)
    active_b = active.astype(jnp.bfloat16)
    result = ((resid + matmul(active_b, weight_down) + bias_down.astype(jnp.float32)) * live_col).astype(jnp.bfloat16)
    gain_one, shift_one, weight_qkv, bias_query, bias_value, weight_out, bias_out, gain_two, shift_two, weight_up, bias_up, weight_down, bias_down = backward_params
    grad_out = block_cot.astype(jnp.float32) * live_col
    grad_out_b = grad_out.astype(jnp.bfloat16)
    grad_wdown = matmul(active_b.T, grad_out_b)
    grad_bdown = lax.optimization_barrier(jnp.sum(grad_out, 0))
    grad_upper = gelu_pull(matmul(grad_out_b, weight_down.T))[0]
    grad_upper_b = grad_upper.astype(jnp.bfloat16)
    grad_wup = matmul(hidden_two.T, grad_upper_b)
    grad_bup = lax.optimization_barrier(jnp.sum(grad_upper, 0))
    grad_hidden_two = matmul(grad_upper_b, weight_up.T)
    grad_resid_norm, grad_gain_two, grad_shift_two = norm_backward(grad_hidden_two, normed_two, inverse_two, gain_two.astype(jnp.float32))
    grad_resid = grad_out + grad_resid_norm
    grad_resid_b = grad_resid.astype(jnp.bfloat16)
    grad_wout = matmul(context.T, grad_resid_b)
    grad_bout = lax.optimization_barrier(jnp.sum(grad_resid, 0))
    grad_context = matmul(grad_resid_b, weight_out.T).astype(jnp.bfloat16).reshape(row_count, head_count, HEAD_DIM)
    probs_again = jnp.exp(score_block(query, keys, allowed) - logsum)
    probs_again_b = probs_again.astype(jnp.bfloat16)
    grad_probs = contract('qhd,khd->hqk', grad_context, value)
    delta = lax.optimization_barrier(jnp.sum(probs_again * grad_probs, -1, keepdims=True))
    grad_scores = (probs_again * (grad_probs - delta) * HEAD_DIM ** (-0.5)).astype(jnp.bfloat16)
    grad_query = contract('hqk,khd->qhd', grad_scores, keys).reshape(row_count, width)
    grad_keys = contract('hqk,qhd->khd', grad_scores, query).reshape(row_count, width)
    grad_value = contract('hqk,qhd->khd', probs_again_b, grad_context).reshape(row_count, width)
    grad_qkv = jnp.concatenate([grad_query, grad_keys, grad_value], 1).astype(jnp.bfloat16)
    grad_bquery = lax.optimization_barrier(jnp.sum(grad_query, 0))
    grad_bvalue = lax.optimization_barrier(jnp.sum(grad_value, 0))
    grad_wqkv = matmul(hidden_one.T, grad_qkv)
    grad_hidden_one = matmul(grad_qkv, weight_qkv.T)
    grad_in_norm, grad_gain_one, grad_shift_one = norm_backward(grad_hidden_one, normed_one, inverse_one, gain_one.astype(jnp.float32))
    grad_in = (grad_resid + grad_in_norm).astype(jnp.bfloat16)
    gradients = (grad_gain_one, grad_shift_one, grad_wqkv, grad_bquery, grad_bvalue, grad_wout, grad_bout, grad_gain_two, grad_shift_two, grad_wup, grad_bup, grad_wdown, grad_bdown)
    return (result, grad_in, gradients)

def reference(tokens_in, cotangent, seq_lengths, live_counts, ln1_gain, ln1_shift, w_qkv, q_bias, v_bias, w_out, out_bias, ln2_gain, ln2_shift, w_up, up_bias, w_down, down_bias):
    params = (ln1_gain, ln1_shift, w_qkv, q_bias, v_bias, w_out, out_bias, ln2_gain, ln2_shift, w_up, up_bias, w_down, down_bias)
    width = tokens_in.shape[1]
    blocks_in = tokens_in.reshape(DEVS, TOK_DEV, width)
    blocks_cot = cotangent.reshape(DEVS, TOK_DEV, width)

    def step_block(totals, items):
        block_in, block_cot, length_row, live_count = items
        result, grad_in, gradients = layer_pass(block_in, block_cot, length_row, live_count, params, params)
        summed = jax.tree.map(lambda running, added: running + added, totals, gradients)
        return (summed, (result, grad_in))
    starting = jax.tree.map(lambda param: jnp.zeros(param.shape, jnp.float32), params)
    totals, (results, grads_in) = lax.scan(step_block, starting, (blocks_in, blocks_cot, seq_lengths, live_counts))
    return (results.reshape(TOKENS, width), grads_in.reshape(TOKENS, width), totals[0], totals[1], totals[2], totals[3], totals[4], totals[5], totals[6], totals[7], totals[8], totals[9], totals[10], totals[11], totals[12])
```

```python
import functools

import jax
import jax.numpy as jnp
from jax import lax
from jax.sharding import PartitionSpec as P

HEAD_DIM = 64


epsilon_norm = 1e-05
masked_score = -1e30


def matmul(left, right):
    return jnp.dot(left, right, preferred_element_type=jnp.float32)


def contract(form, left, right):
    return jnp.einsum(form, left, right, preferred_element_type=jnp.float32)


def norm_forward(values, gain, shift):
    center = values - jnp.mean(values, -1, keepdims=True)
    inverse = lax.rsqrt(jnp.mean(center * center, -1, keepdims=True) + epsilon_norm)
    normed = center * inverse
    return (normed * gain + shift, normed, inverse)


def norm_backward(upstream, normed, inverse, gain):
    scaled = upstream * gain
    inward = inverse * (
        scaled
        - jnp.mean(scaled, -1, keepdims=True)
        - normed * jnp.mean(scaled * normed, -1, keepdims=True)
    )
    return (inward, jnp.sum(upstream * normed, 0), jnp.sum(upstream, 0))


def live_mask(length_row, live_count, row_count):
    position = jnp.arange(row_count, dtype=jnp.int32)
    bounds = jnp.cumsum(length_row)
    segment = jnp.sum((position[:, None] >= bounds[None, :]).astype(jnp.int32), 1)
    live = position < live_count
    allowed = (segment[:, None] == segment[None, :]) & (position[None, :] <= position[:, None])
    allowed = allowed & (live[None, :] | (position[:, None] == position[None, :]))
    return (allowed, live)


def gelu_tanh(values):
    return jax.nn.gelu(values, approximate=True)


def score_block(query, keys, allowed):
    scores = contract("qhd,khd->hqk", query, keys) * query.shape[-1] ** (-0.5)
    return jnp.where(allowed[None], scores, masked_score)


def layer_pass(block_in, block_cot, length_row, live_count, forward_params, backward_params):
    (
        gain_one,
        shift_one,
        weight_qkv,
        bias_query,
        bias_value,
        weight_out,
        bias_out,
        gain_two,
        shift_two,
        weight_up,
        bias_up,
        weight_down,
        bias_down,
    ) = forward_params
    row_count = block_in.shape[0]
    width = block_in.shape[1]
    head_count = width // HEAD_DIM
    allowed, live = live_mask(length_row, live_count, row_count)
    live_col = live[:, None].astype(jnp.float32)
    tokens_f = block_in.astype(jnp.float32)
    normed_in, normed_one, inverse_one = norm_forward(
        tokens_f, gain_one.astype(jnp.float32), shift_one.astype(jnp.float32)
    )
    hidden_one = normed_in.astype(jnp.bfloat16)
    bias_full = jnp.concatenate(
        [
            bias_query.astype(jnp.float32),
            jnp.zeros((width,), jnp.float32),
            bias_value.astype(jnp.float32),
        ]
    )
    qkv = (matmul(hidden_one, weight_qkv) + bias_full).astype(jnp.bfloat16)
    query = qkv[:, :width].reshape(row_count, head_count, HEAD_DIM)
    keys = qkv[:, width : 2 * width].reshape(row_count, head_count, HEAD_DIM)
    value = qkv[:, 2 * width :].reshape(row_count, head_count, HEAD_DIM)
    scores = score_block(query, keys, allowed)
    highest = jnp.max(scores, -1, keepdims=True)
    logsum = highest + jnp.log(jnp.sum(jnp.exp(scores - highest), -1, keepdims=True))
    probs_b = jnp.exp(scores - logsum).astype(jnp.bfloat16)
    context = (
        contract("hqk,khd->qhd", probs_b, value).reshape(row_count, width).astype(jnp.bfloat16)
    )
    resid = tokens_f + matmul(context, weight_out) + bias_out.astype(jnp.float32)
    normed_mid, normed_two, inverse_two = norm_forward(
        resid, gain_two.astype(jnp.float32), shift_two.astype(jnp.float32)
    )
    hidden_two = normed_mid.astype(jnp.bfloat16)
    upper = matmul(hidden_two, weight_up) + bias_up.astype(jnp.float32)
    active, gelu_pull = jax.vjp(gelu_tanh, upper)
    active_b = active.astype(jnp.bfloat16)
    result = (
        (resid + matmul(active_b, weight_down) + bias_down.astype(jnp.float32)) * live_col
    ).astype(jnp.bfloat16)
    (
        gain_one,
        shift_one,
        weight_qkv,
        bias_query,
        bias_value,
        weight_out,
        bias_out,
        gain_two,
        shift_two,
        weight_up,
        bias_up,
        weight_down,
        bias_down,
    ) = backward_params
    grad_out = block_cot.astype(jnp.float32) * live_col
    grad_out_b = grad_out.astype(jnp.bfloat16)
    grad_wdown = matmul(active_b.T, grad_out_b)
    grad_bdown = jnp.sum(grad_out, 0)
    grad_upper = gelu_pull(matmul(grad_out_b, weight_down.T))[0]
    grad_upper_b = grad_upper.astype(jnp.bfloat16)
    grad_wup = matmul(hidden_two.T, grad_upper_b)
    grad_bup = jnp.sum(grad_upper, 0)
    grad_hidden_two = matmul(grad_upper_b, weight_up.T)
    grad_resid_norm, grad_gain_two, grad_shift_two = norm_backward(
        grad_hidden_two, normed_two, inverse_two, gain_two.astype(jnp.float32)
    )
    grad_resid = grad_out + grad_resid_norm
    grad_resid_b = grad_resid.astype(jnp.bfloat16)
    grad_wout = matmul(context.T, grad_resid_b)
    grad_bout = jnp.sum(grad_resid, 0)
    grad_context = (
        matmul(grad_resid_b, weight_out.T)
        .astype(jnp.bfloat16)
        .reshape(row_count, head_count, HEAD_DIM)
    )
    probs_again = jnp.exp(score_block(query, keys, allowed) - logsum)
    probs_again_b = probs_again.astype(jnp.bfloat16)
    grad_probs = contract("qhd,khd->hqk", grad_context, value)
    delta = jnp.sum(probs_again * grad_probs, -1, keepdims=True)
    grad_scores = (probs_again * (grad_probs - delta) * HEAD_DIM ** (-0.5)).astype(jnp.bfloat16)
    grad_query = contract("hqk,khd->qhd", grad_scores, keys).reshape(row_count, width)
    grad_keys = contract("hqk,qhd->khd", grad_scores, query).reshape(row_count, width)
    grad_value = contract("hqk,qhd->khd", probs_again_b, grad_context).reshape(row_count, width)
    grad_qkv = jnp.concatenate([grad_query, grad_keys, grad_value], 1).astype(jnp.bfloat16)
    grad_bquery = jnp.sum(grad_query, 0)
    grad_bvalue = jnp.sum(grad_value, 0)
    grad_wqkv = matmul(hidden_one.T, grad_qkv)
    grad_hidden_one = matmul(grad_qkv, weight_qkv.T)
    grad_in_norm, grad_gain_one, grad_shift_one = norm_backward(
        grad_hidden_one, normed_one, inverse_one, gain_one.astype(jnp.float32)
    )
    grad_in = (grad_resid + grad_in_norm).astype(jnp.bfloat16)
    gradients = (
        grad_gain_one,
        grad_shift_one,
        grad_wqkv,
        grad_bquery,
        grad_bvalue,
        grad_wout,
        grad_bout,
        grad_gain_two,
        grad_shift_two,
        grad_wup,
        grad_bup,
        grad_wdown,
        grad_bdown,
    )
    return (result, grad_in, gradients)


def plain_local(
    tokens_in,
    cotangent,
    seq_lengths,
    live_counts,
    ln1_gain,
    ln1_shift,
    w_qkv,
    q_bias,
    v_bias,
    w_out,
    out_bias,
    ln2_gain,
    ln2_shift,
    w_up,
    up_bias,
    w_down,
    down_bias,
):
    forward_params = (
        lax.all_gather(ln1_gain, "shard", axis=0, tiled=True),
        lax.all_gather(ln1_shift, "shard", axis=0, tiled=True),
        lax.all_gather(w_qkv, "shard", axis=0, tiled=True),
        lax.all_gather(q_bias, "shard", axis=0, tiled=True),
        lax.all_gather(v_bias, "shard", axis=0, tiled=True),
        lax.all_gather(w_out, "shard", axis=0, tiled=True),
        lax.all_gather(out_bias, "shard", axis=0, tiled=True),
        lax.all_gather(ln2_gain, "shard", axis=0, tiled=True),
        lax.all_gather(ln2_shift, "shard", axis=0, tiled=True),
        lax.all_gather(w_up, "shard", axis=1, tiled=True),
        lax.all_gather(up_bias, "shard", axis=0, tiled=True),
        lax.all_gather(w_down, "shard", axis=0, tiled=True),
        lax.all_gather(down_bias, "shard", axis=0, tiled=True),
    )
    backward_params = (
        lax.all_gather(ln1_gain, "shard", axis=0, tiled=True),
        lax.all_gather(ln1_shift, "shard", axis=0, tiled=True),
        lax.all_gather(w_qkv, "shard", axis=0, tiled=True),
        lax.all_gather(q_bias, "shard", axis=0, tiled=True),
        lax.all_gather(v_bias, "shard", axis=0, tiled=True),
        lax.all_gather(w_out, "shard", axis=0, tiled=True),
        lax.all_gather(out_bias, "shard", axis=0, tiled=True),
        lax.all_gather(ln2_gain, "shard", axis=0, tiled=True),
        lax.all_gather(ln2_shift, "shard", axis=0, tiled=True),
        lax.all_gather(w_up, "shard", axis=1, tiled=True),
        lax.all_gather(up_bias, "shard", axis=0, tiled=True),
        lax.all_gather(w_down, "shard", axis=0, tiled=True),
        lax.all_gather(down_bias, "shard", axis=0, tiled=True),
    )
    result, grad_in, gradients = layer_pass(
        tokens_in, cotangent, seq_lengths[0], live_counts[0], forward_params, backward_params
    )
    (
        grad_gain_one,
        grad_shift_one,
        grad_wqkv,
        grad_bquery,
        grad_bvalue,
        grad_wout,
        grad_bout,
        grad_gain_two,
        grad_shift_two,
        grad_wup,
        grad_bup,
        grad_wdown,
        grad_bdown,
    ) = gradients
    owned = (
        lax.psum_scatter(grad_gain_one, "shard", scatter_dimension=0, tiled=True),
        lax.psum_scatter(grad_shift_one, "shard", scatter_dimension=0, tiled=True),
        lax.psum_scatter(grad_wqkv, "shard", scatter_dimension=0, tiled=True),
        lax.psum_scatter(grad_bquery, "shard", scatter_dimension=0, tiled=True),
        lax.psum_scatter(grad_bvalue, "shard", scatter_dimension=0, tiled=True),
        lax.psum_scatter(grad_wout, "shard", scatter_dimension=0, tiled=True),
        lax.psum_scatter(grad_bout, "shard", scatter_dimension=0, tiled=True),
        lax.psum_scatter(grad_gain_two, "shard", scatter_dimension=0, tiled=True),
        lax.psum_scatter(grad_shift_two, "shard", scatter_dimension=0, tiled=True),
        lax.psum_scatter(grad_wup, "shard", scatter_dimension=1, tiled=True),
        lax.psum_scatter(grad_bup, "shard", scatter_dimension=0, tiled=True),
        lax.psum_scatter(grad_wdown, "shard", scatter_dimension=0, tiled=True),
        lax.psum_scatter(grad_bdown, "shard", scatter_dimension=0, tiled=True),
    )
    (
        owned_gain_one,
        owned_shift_one,
        owned_wqkv,
        owned_bquery,
        owned_bvalue,
        owned_wout,
        owned_bout,
        owned_gain_two,
        owned_shift_two,
        owned_wup,
        owned_bup,
        owned_wdown,
        owned_bdown,
    ) = owned
    summed = lax.psum(
        (
            owned_gain_one,
            owned_shift_one,
            owned_wqkv,
            owned_bquery,
            owned_bvalue,
            owned_wout,
            owned_bout,
            owned_gain_two,
            owned_shift_two,
            owned_wup,
            owned_bup,
            owned_wdown,
            owned_bdown,
        ),
        "rep",
    )
    return (result, grad_in) + tuple(summed)


def exchange(array, axis, distance, size):
    return lax.ppermute(array, axis, [(i, i ^ distance) for i in range(size)])


def halve(array, bit, distance, size):
    rows = array.shape[0] // 2
    send = lax.dynamic_slice_in_dim(array, (1 - bit) * rows, rows, 0)
    keep = lax.dynamic_slice_in_dim(array, bit * rows, rows, 0)
    return keep + exchange(send, "rep", distance, size)


def double(array, bit, distance, size, dtype):
    other = exchange(array, "rep", distance, size)
    low = jnp.where(bit == 0, array, other).astype(dtype)
    high = jnp.where(bit == 0, other, array).astype(dtype)
    return jnp.concatenate([low, high], 0)


def rep_sum(array, order, size):
    place = lax.axis_index("rep")
    for distance in order:
        array = halve(array, (place // distance) % 2, distance, size)
    for distance in reversed(order):
        last = distance == order[0]
        array = double(
            array, (place // distance) % 2, distance, size, jnp.float32 if last else array.dtype
        )
    return array


def small_sum(array, size):
    distance = 1
    while distance < size:
        array = array + exchange(array, "rep", distance, size)
        distance *= 2
    return array


def pair_local(
    tokens_in,
    cotangent,
    seq_lengths,
    live_counts,
    ln1_gain,
    ln1_shift,
    w_qkv,
    q_bias,
    v_bias,
    w_out,
    out_bias,
    ln2_gain,
    ln2_shift,
    w_up,
    up_bias,
    w_down,
    down_bias,
    reps,
):
    core = lax.axis_index("shard")
    first = core == 0

    def swap(array):
        return exchange(array, "shard", 1, 2)

    def natural(own, other, dim):
        return jnp.concatenate([jnp.where(first, own, other), jnp.where(first, other, own)], dim)

    def own_first(array, dim):
        low, high = jnp.split(array, 2, dim)
        return jnp.concatenate([jnp.where(first, low, high), jnp.where(first, high, low)], dim)

    def f32(array):
        return array.astype(jnp.float32)

    rows, width = tokens_in.shape
    half = width // 2
    heads = half // HEAD_DIM
    hidden = w_up.shape[1]
    w_parts = w_qkv.reshape(half, 3, 2, half)
    w_mine = jnp.where(first, w_parts[:, :, 0], w_parts[:, :, 1]).reshape(half, 3 * half)
    w_theirs = jnp.where(first, w_parts[:, :, 1], w_parts[:, :, 0]).reshape(half, 3 * half)
    tokens_other = swap(tokens_in)
    w_cols = jnp.concatenate([w_mine, swap(w_theirs)], 0)
    numbers = jnp.concatenate([seq_lengths[0], live_counts])
    numbers_other = swap(numbers)
    vectors = jnp.stack([ln1_gain, ln1_shift, out_bias, ln2_gain, ln2_shift, down_bias])
    gain_one, shift_one, bias_out, gain_two, shift_two, bias_down = f32(
        natural(vectors, swap(vectors), 1)
    )
    w_out_rows = jnp.concatenate([w_out, swap(w_out)], 0)
    cot_two = jnp.concatenate([cotangent, swap(cotangent)], 0)
    masks = [live_mask(n[:-1], n[-1], rows) for n in (numbers, numbers_other)]
    allowed = jnp.stack([m[0] for m in masks])
    live = jnp.concatenate([m[1] for m in masks])
    live_col = f32(live)[:, None]
    tokens_f = f32(jnp.concatenate([tokens_in, tokens_other], 0))
    normed_in, normed_one, inverse_one = norm_forward(tokens_f, gain_one, shift_one)
    hidden_one = own_first(normed_in.astype(jnp.bfloat16), 1)
    bias_full = jnp.concatenate([f32(q_bias), jnp.zeros((half,), jnp.float32), f32(v_bias)])
    qkv = (matmul(hidden_one, w_cols) + bias_full).astype(jnp.bfloat16)
    query, keys, value = [
        part.reshape(2, rows, heads, HEAD_DIM) for part in jnp.split(qkv, 3, 1)
    ]

    def score():
        scores = contract("bqhd,bkhd->bhqk", query, keys) * HEAD_DIM ** (-0.5)
        return jnp.where(allowed[:, None], scores, masked_score)

    scores = score()
    highest = jnp.max(scores, -1, keepdims=True)
    logsum = highest + jnp.log(jnp.sum(jnp.exp(scores - highest), -1, keepdims=True))
    probs = jnp.exp(scores - logsum)
    probs_b = probs.astype(jnp.bfloat16)
    context = (
        contract("bhqk,bkhd->bqhd", probs_b, value).reshape(2 * rows, half).astype(jnp.bfloat16)
    )
    context_turned = jnp.concatenate([context[rows:], context[:rows]], 0)
    context_all = jnp.concatenate([context, swap(context_turned)], 1)
    resid = tokens_f + matmul(context_all, w_out_rows) + bias_out
    normed_mid, normed_two, inverse_two = norm_forward(resid, gain_two, shift_two)
    hidden_two = normed_mid.astype(jnp.bfloat16)
    grad_out = f32(cot_two) * live_col
    grad_out_b = grad_out.astype(jnp.bfloat16)
    pieces = 2
    step = hidden // pieces
    down, grad_hidden = 0.0, 0.0
    downs, ups, bias_ups = [], [], []
    for i in range(pieces):
        cut = slice(i * step, (i + 1) * step)
        upper = matmul(hidden_two, w_up[:, cut]) + f32(up_bias[cut])
        active, gelu_pull = jax.vjp(gelu_tanh, upper)
        active_b = active.astype(jnp.bfloat16)
        downs.append(matmul(active_b.T, grad_out_b).astype(jnp.bfloat16))
        grad_upper = gelu_pull(matmul(grad_out_b, w_down[cut].T))[0]
        grad_upper_b = grad_upper.astype(jnp.bfloat16)
        ups.append(matmul(hidden_two.T, grad_upper_b).astype(jnp.bfloat16))
        bias_ups.append(jnp.sum(grad_upper, 0))
        down = down + matmul(active_b, w_down[cut])
        grad_hidden = grad_hidden + matmul(grad_upper_b, w_up[:, cut].T)
    grad_hidden_two = grad_hidden[:rows] + swap(grad_hidden[rows:])
    result = (
        (resid[:rows] + down[:rows] + swap(down[rows:]) + bias_down) * live_col[:rows]
    ).astype(jnp.bfloat16)
    grad_bdown = jnp.sum(grad_out[:rows], 0)
    grad_resid_norm, grad_gain_two, grad_shift_two = norm_backward(
        grad_hidden_two, normed_two[:rows], inverse_two[:rows], gain_two
    )
    grad_resid = grad_out[:rows] + grad_resid_norm
    grad_resid_b = grad_resid.astype(jnp.bfloat16)
    grad_resid_two = jnp.concatenate([grad_resid_b, swap(grad_resid_b)], 0)
    grad_bout = jnp.sum(grad_resid, 0)
    grad_wout = matmul(context.T, grad_resid_two).astype(jnp.bfloat16)
    grad_context = (
        matmul(grad_resid_two, w_out.T).astype(jnp.bfloat16).reshape(2, rows, heads, HEAD_DIM)
    )
    grad_probs = contract("bqhd,bkhd->bhqk", grad_context, value)
    delta = jnp.sum(probs * grad_probs, -1, keepdims=True)
    grad_scores = (probs * (grad_probs - delta) * HEAD_DIM ** (-0.5)).astype(jnp.bfloat16)
    flat = (2 * rows, half)
    grad_query = contract("bhqk,bkhd->bqhd", grad_scores, keys).reshape(flat)
    grad_keys = contract("bhqk,bqhd->bkhd", grad_scores, query).reshape(flat)
    grad_value = contract("bhqk,bqhd->bkhd", probs_b, grad_context).reshape(flat)
    grad_qkv = jnp.concatenate([grad_query, grad_keys, grad_value], 1).astype(jnp.bfloat16)
    theirs = matmul(hidden_one[:, half:].T, grad_qkv).astype(jnp.bfloat16)
    mine = matmul(hidden_one[:, :half].T, grad_qkv).astype(jnp.bfloat16)
    grad_wqkv = jnp.concatenate([mine, swap(theirs)], 0)
    grad_one = own_first(matmul(grad_qkv, w_cols.T), 1)
    grad_hidden_one = grad_one[:rows] + swap(grad_one[rows:])
    grad_in_norm, grad_gain_one, grad_shift_one = norm_backward(
        grad_hidden_one, normed_one[:rows], inverse_one[:rows], gain_one
    )
    grad_in = (grad_resid + grad_in_norm).astype(jnp.bfloat16)
    orders = rep_orders(reps)
    sum_downs = [rep_sum(downs[0], orders[0], reps), rep_sum(downs[1], orders[1], reps)]
    sum_ups = [rep_sum(ups[0], orders[1], reps), rep_sum(ups[1], orders[0], reps)]
    sum_wout = rep_sum(grad_wout, orders[0], reps)
    sum_wqkv = rep_sum(grad_wqkv, orders[2], reps)
    wide = jnp.stack(
        [grad_gain_one, grad_shift_one, grad_bout, grad_gain_two, grad_shift_two, grad_bdown]
    )
    wide = own_first(wide, 1)
    pack = jnp.concatenate(
        [
            wide[:, :half] + swap(wide[:, half:]),
            jnp.sum(grad_query, 0)[None],
            jnp.sum(grad_value, 0)[None],
            jnp.concatenate(bias_ups).reshape(-1, half),
        ],
        0,
    )
    pack = small_sum(pack, reps)
    own_cols, other_cols = [part.reshape(half, 3, 1, half) for part in jnp.split(sum_wqkv, 2, 0)]
    return (
        result,
        grad_in,
        pack[0],
        pack[1],
        natural(own_cols, other_cols, 2).reshape(half, 3 * width),
        pack[6],
        pack[7],
        sum_wout,
        pack[2],
        pack[3],
        pack[4],
        jnp.concatenate(sum_ups, 1),
        pack[8:].reshape(-1),
        jnp.concatenate(sum_downs, 0),
        pack[5],
    )


def rep_orders(reps):
    bits = [1 << i for i in range(reps.bit_length() - 1)]
    return (bits, bits[1::-1] + bits[2:], bits[2:] + bits[:2])


def pair_fits(mesh):
    reps = mesh.shape["rep"]
    return mesh.shape["shard"] == 2 and reps >= 4 and reps & (reps - 1) == 0


def solution(mesh):
    local = plain_local
    if pair_fits(mesh):
        local = functools.partial(pair_local, reps=mesh.shape["rep"])
    return jax.shard_map(
        local,
        mesh=mesh,
        in_specs=(
            P(("rep", "shard"), None),
            P(("rep", "shard"), None),
            P(("rep", "shard"), None),
            P(("rep", "shard")),
            P("shard"),
            P("shard"),
            P("shard", None),
            P("shard"),
            P("shard"),
            P("shard", None),
            P("shard"),
            P("shard"),
            P("shard"),
            P(None, "shard"),
            P("shard"),
            P("shard", None),
            P("shard"),
        ),
        out_specs=(
            P(("rep", "shard"), None),
            P(("rep", "shard"), None),
            P("shard"),
            P("shard"),
            P("shard", None),
            P("shard"),
            P("shard"),
            P("shard", None),
            P("shard"),
            P("shard"),
            P("shard"),
            P(None, "shard"),
            P("shard"),
            P("shard", None),
            P("shard"),
        ),
        check_vma=False,
    )
```

```python
import functools
import math

import jax
import jax.numpy as jnp
from jax import lax
from jax.experimental import pallas as pl
from jax.experimental.pallas import tpu as pltpu
from jax.sharding import PartitionSpec as P

HEAD_DIM = 64


epsilon_norm = 1e-05
masked_score = -1e30


def matmul(left, right):
    return jnp.dot(left, right, preferred_element_type=jnp.float32)


def contract(form, left, right):
    return jnp.einsum(form, left, right, preferred_element_type=jnp.float32)


def norm_forward(values, gain, shift):
    center = values - jnp.mean(values, -1, keepdims=True)
    inverse = lax.rsqrt(jnp.mean(center * center, -1, keepdims=True) + epsilon_norm)
    normed = center * inverse
    return (normed * gain + shift, normed, inverse)


def norm_backward(upstream, normed, inverse, gain):
    scaled = upstream * gain
    inward = inverse * (
        scaled
        - jnp.mean(scaled, -1, keepdims=True)
        - normed * jnp.mean(scaled * normed, -1, keepdims=True)
    )
    return (inward, jnp.sum(upstream * normed, 0), jnp.sum(upstream, 0))


def live_mask(length_row, live_count, row_count):
    position = jnp.arange(row_count, dtype=jnp.int32)
    bounds = jnp.cumsum(length_row)
    segment = jnp.sum((position[:, None] >= bounds[None, :]).astype(jnp.int32), 1)
    live = position < live_count
    allowed = (segment[:, None] == segment[None, :]) & (position[None, :] <= position[:, None])
    allowed = allowed & (live[None, :] | (position[:, None] == position[None, :]))
    return (allowed, live)


def gelu_tanh(values):
    return jax.nn.gelu(values, approximate=True)


def score_block(query, keys, allowed):
    scores = contract("qhd,khd->hqk", query, keys) * query.shape[-1] ** (-0.5)
    return jnp.where(allowed[None], scores, masked_score)


def layer_pass(block_in, block_cot, length_row, live_count, forward_params, backward_params):
    (
        gain_one,
        shift_one,
        weight_qkv,
        bias_query,
        bias_value,
        weight_out,
        bias_out,
        gain_two,
        shift_two,
        weight_up,
        bias_up,
        weight_down,
        bias_down,
    ) = forward_params
    row_count = block_in.shape[0]
    width = block_in.shape[1]
    head_count = width // HEAD_DIM
    allowed, live = live_mask(length_row, live_count, row_count)
    live_col = live[:, None].astype(jnp.float32)
    tokens_f = block_in.astype(jnp.float32)
    normed_in, normed_one, inverse_one = norm_forward(
        tokens_f, gain_one.astype(jnp.float32), shift_one.astype(jnp.float32)
    )
    hidden_one = normed_in.astype(jnp.bfloat16)
    bias_full = jnp.concatenate(
        [
            bias_query.astype(jnp.float32),
            jnp.zeros((width,), jnp.float32),
            bias_value.astype(jnp.float32),
        ]
    )
    qkv = (matmul(hidden_one, weight_qkv) + bias_full).astype(jnp.bfloat16)
    query = qkv[:, :width].reshape(row_count, head_count, HEAD_DIM)
    keys = qkv[:, width : 2 * width].reshape(row_count, head_count, HEAD_DIM)
    value = qkv[:, 2 * width :].reshape(row_count, head_count, HEAD_DIM)
    scores = score_block(query, keys, allowed)
    highest = jnp.max(scores, -1, keepdims=True)
    logsum = highest + jnp.log(jnp.sum(jnp.exp(scores - highest), -1, keepdims=True))
    probs_b = jnp.exp(scores - logsum).astype(jnp.bfloat16)
    context = (
        contract("hqk,khd->qhd", probs_b, value).reshape(row_count, width).astype(jnp.bfloat16)
    )
    resid = tokens_f + matmul(context, weight_out) + bias_out.astype(jnp.float32)
    normed_mid, normed_two, inverse_two = norm_forward(
        resid, gain_two.astype(jnp.float32), shift_two.astype(jnp.float32)
    )
    hidden_two = normed_mid.astype(jnp.bfloat16)
    upper = matmul(hidden_two, weight_up) + bias_up.astype(jnp.float32)
    active, gelu_pull = jax.vjp(gelu_tanh, upper)
    active_b = active.astype(jnp.bfloat16)
    result = (
        (resid + matmul(active_b, weight_down) + bias_down.astype(jnp.float32)) * live_col
    ).astype(jnp.bfloat16)
    (
        gain_one,
        shift_one,
        weight_qkv,
        bias_query,
        bias_value,
        weight_out,
        bias_out,
        gain_two,
        shift_two,
        weight_up,
        bias_up,
        weight_down,
        bias_down,
    ) = backward_params
    grad_out = block_cot.astype(jnp.float32) * live_col
    grad_out_b = grad_out.astype(jnp.bfloat16)
    grad_wdown = matmul(active_b.T, grad_out_b)
    grad_bdown = jnp.sum(grad_out, 0)
    grad_upper = gelu_pull(matmul(grad_out_b, weight_down.T))[0]
    grad_upper_b = grad_upper.astype(jnp.bfloat16)
    grad_wup = matmul(hidden_two.T, grad_upper_b)
    grad_bup = jnp.sum(grad_upper, 0)
    grad_hidden_two = matmul(grad_upper_b, weight_up.T)
    grad_resid_norm, grad_gain_two, grad_shift_two = norm_backward(
        grad_hidden_two, normed_two, inverse_two, gain_two.astype(jnp.float32)
    )
    grad_resid = grad_out + grad_resid_norm
    grad_resid_b = grad_resid.astype(jnp.bfloat16)
    grad_wout = matmul(context.T, grad_resid_b)
    grad_bout = jnp.sum(grad_resid, 0)
    grad_context = (
        matmul(grad_resid_b, weight_out.T)
        .astype(jnp.bfloat16)
        .reshape(row_count, head_count, HEAD_DIM)
    )
    probs_again = jnp.exp(score_block(query, keys, allowed) - logsum)
    probs_again_b = probs_again.astype(jnp.bfloat16)
    grad_probs = contract("qhd,khd->hqk", grad_context, value)
    delta = jnp.sum(probs_again * grad_probs, -1, keepdims=True)
    grad_scores = (probs_again * (grad_probs - delta) * HEAD_DIM ** (-0.5)).astype(jnp.bfloat16)
    grad_query = contract("hqk,khd->qhd", grad_scores, keys).reshape(row_count, width)
    grad_keys = contract("hqk,qhd->khd", grad_scores, query).reshape(row_count, width)
    grad_value = contract("hqk,qhd->khd", probs_again_b, grad_context).reshape(row_count, width)
    grad_qkv = jnp.concatenate([grad_query, grad_keys, grad_value], 1).astype(jnp.bfloat16)
    grad_bquery = jnp.sum(grad_query, 0)
    grad_bvalue = jnp.sum(grad_value, 0)
    grad_wqkv = matmul(hidden_one.T, grad_qkv)
    grad_hidden_one = matmul(grad_qkv, weight_qkv.T)
    grad_in_norm, grad_gain_one, grad_shift_one = norm_backward(
        grad_hidden_one, normed_one, inverse_one, gain_one.astype(jnp.float32)
    )
    grad_in = (grad_resid + grad_in_norm).astype(jnp.bfloat16)
    gradients = (
        grad_gain_one,
        grad_shift_one,
        grad_wqkv,
        grad_bquery,
        grad_bvalue,
        grad_wout,
        grad_bout,
        grad_gain_two,
        grad_shift_two,
        grad_wup,
        grad_bup,
        grad_wdown,
        grad_bdown,
    )
    return (result, grad_in, gradients)


def plain_local(
    tokens_in,
    cotangent,
    seq_lengths,
    live_counts,
    ln1_gain,
    ln1_shift,
    w_qkv,
    q_bias,
    v_bias,
    w_out,
    out_bias,
    ln2_gain,
    ln2_shift,
    w_up,
    up_bias,
    w_down,
    down_bias,
):
    forward_params = (
        lax.all_gather(ln1_gain, "shard", axis=0, tiled=True),
        lax.all_gather(ln1_shift, "shard", axis=0, tiled=True),
        lax.all_gather(w_qkv, "shard", axis=0, tiled=True),
        lax.all_gather(q_bias, "shard", axis=0, tiled=True),
        lax.all_gather(v_bias, "shard", axis=0, tiled=True),
        lax.all_gather(w_out, "shard", axis=0, tiled=True),
        lax.all_gather(out_bias, "shard", axis=0, tiled=True),
        lax.all_gather(ln2_gain, "shard", axis=0, tiled=True),
        lax.all_gather(ln2_shift, "shard", axis=0, tiled=True),
        lax.all_gather(w_up, "shard", axis=1, tiled=True),
        lax.all_gather(up_bias, "shard", axis=0, tiled=True),
        lax.all_gather(w_down, "shard", axis=0, tiled=True),
        lax.all_gather(down_bias, "shard", axis=0, tiled=True),
    )
    backward_params = (
        lax.all_gather(ln1_gain, "shard", axis=0, tiled=True),
        lax.all_gather(ln1_shift, "shard", axis=0, tiled=True),
        lax.all_gather(w_qkv, "shard", axis=0, tiled=True),
        lax.all_gather(q_bias, "shard", axis=0, tiled=True),
        lax.all_gather(v_bias, "shard", axis=0, tiled=True),
        lax.all_gather(w_out, "shard", axis=0, tiled=True),
        lax.all_gather(out_bias, "shard", axis=0, tiled=True),
        lax.all_gather(ln2_gain, "shard", axis=0, tiled=True),
        lax.all_gather(ln2_shift, "shard", axis=0, tiled=True),
        lax.all_gather(w_up, "shard", axis=1, tiled=True),
        lax.all_gather(up_bias, "shard", axis=0, tiled=True),
        lax.all_gather(w_down, "shard", axis=0, tiled=True),
        lax.all_gather(down_bias, "shard", axis=0, tiled=True),
    )
    result, grad_in, gradients = layer_pass(
        tokens_in, cotangent, seq_lengths[0], live_counts[0], forward_params, backward_params
    )
    (
        grad_gain_one,
        grad_shift_one,
        grad_wqkv,
        grad_bquery,
        grad_bvalue,
        grad_wout,
        grad_bout,
        grad_gain_two,
        grad_shift_two,
        grad_wup,
        grad_bup,
        grad_wdown,
        grad_bdown,
    ) = gradients
    owned = (
        lax.psum_scatter(grad_gain_one, "shard", scatter_dimension=0, tiled=True),
        lax.psum_scatter(grad_shift_one, "shard", scatter_dimension=0, tiled=True),
        lax.psum_scatter(grad_wqkv, "shard", scatter_dimension=0, tiled=True),
        lax.psum_scatter(grad_bquery, "shard", scatter_dimension=0, tiled=True),
        lax.psum_scatter(grad_bvalue, "shard", scatter_dimension=0, tiled=True),
        lax.psum_scatter(grad_wout, "shard", scatter_dimension=0, tiled=True),
        lax.psum_scatter(grad_bout, "shard", scatter_dimension=0, tiled=True),
        lax.psum_scatter(grad_gain_two, "shard", scatter_dimension=0, tiled=True),
        lax.psum_scatter(grad_shift_two, "shard", scatter_dimension=0, tiled=True),
        lax.psum_scatter(grad_wup, "shard", scatter_dimension=1, tiled=True),
        lax.psum_scatter(grad_bup, "shard", scatter_dimension=0, tiled=True),
        lax.psum_scatter(grad_wdown, "shard", scatter_dimension=0, tiled=True),
        lax.psum_scatter(grad_bdown, "shard", scatter_dimension=0, tiled=True),
    )
    (
        owned_gain_one,
        owned_shift_one,
        owned_wqkv,
        owned_bquery,
        owned_bvalue,
        owned_wout,
        owned_bout,
        owned_gain_two,
        owned_shift_two,
        owned_wup,
        owned_bup,
        owned_wdown,
        owned_bdown,
    ) = owned
    summed = lax.psum(
        (
            owned_gain_one,
            owned_shift_one,
            owned_wqkv,
            owned_bquery,
            owned_bvalue,
            owned_wout,
            owned_bout,
            owned_gain_two,
            owned_shift_two,
            owned_wup,
            owned_bup,
            owned_wdown,
            owned_bdown,
        ),
        "rep",
    )
    return (result, grad_in) + tuple(summed)


def exchange(array, axis, distance, size):
    return lax.ppermute(array, axis, [(i, i ^ distance) for i in range(size)])


def cross(array, distances, size):
    pairs = [
        (2 * place + core, 2 * (place ^ distance) + core)
        for place in range(size)
        for core, distance in enumerate(distances)
    ]
    return lax.ppermute(array, ("rep", "shard"), pairs)


def rep_sum(keep, send, order, size):
    keep = keep + cross(send, order[0], size)
    for distances in order[1:]:
        count = keep.shape[0] // 2
        keep = keep[:count] + cross(keep[count:], distances, size)
    for distances in reversed(order[1:]):
        keep = jnp.concatenate([keep, cross(keep, distances, size)], 0)
    return keep, cross(keep, order[0], size)


def small_sum(array, size):
    distance = 1
    while distance < size:
        array = array + exchange(array, "rep", distance, size)
        distance *= 2
    return array


def dot_nt(left, right):
    return lax.dot_general(left, right, (((1,), (1,)), ((), ())), preferred_element_type=jnp.float32)


def dot_tn(left, right):
    return lax.dot_general(left, right, (((0,), (0,)), ((), ())), preferred_element_type=jnp.float32)


def f32(array):
    return array.astype(jnp.float32)


def bf16(array):
    return array.astype(jnp.bfloat16)


def lanes(offset, size):
    return pl.ds(pl.multiple_of(offset, 128), size)


def call(kernel, outs, operands, scalars, scratch=(), flops=0):
    return pl.pallas_call(
        kernel,
        out_shape=[jax.ShapeDtypeStruct(shape, dtype) for shape, dtype in outs],
        in_specs=[pl.BlockSpec(memory_space=pltpu.SMEM)] * scalars
        + [pl.BlockSpec(memory_space=pltpu.VMEM)] * (len(operands) - scalars),
        out_specs=[pl.BlockSpec(memory_space=pltpu.VMEM)] * len(outs),
        scratch_shapes=list(scratch),
        compiler_params=pltpu.CompilerParams(vmem_limit_bytes=48 << 20),
        cost_estimate=pl.CostEstimate(flops=flops, transcendentals=0, bytes_accessed=8 << 20),
    )(*operands)


def allowed_pairs(numbers, block, rows):
    row = lax.broadcasted_iota(jnp.int32, (rows, rows), 0)
    col = lax.broadcasted_iota(jnp.int32, (rows, rows), 1)
    row_segment, col_segment = jnp.zeros_like(row), jnp.zeros_like(col)
    bound = 0
    last = numbers.shape[1] - 1
    for i in range(last):
        bound = bound + numbers[block, i]
        row_segment = row_segment + (row >= bound).astype(jnp.int32)
        col_segment = col_segment + (col >= bound).astype(jnp.int32)
    same = (row_segment == col_segment) & (col <= row)
    return same & ((col < numbers[block, last]) | (row == col))


def head_probs(query, keys, allowed):
    scores = dot_nt(query, keys) * HEAD_DIM ** (-0.5)
    scores = jnp.where(allowed, scores, masked_score)
    powers = jnp.exp(scores - jnp.max(scores, -1, keepdims=True))
    return powers / jnp.sum(powers, -1, keepdims=True)


def attention_forward(
    place, numbers, tokens, tokens_other, w_own, w_other, v_own, v_other, hidden, qkv, context, normed
):
    core = place[2]
    rows, width = tokens.shape
    half = width // 2
    for block, ref in enumerate((tokens, tokens_other)):
        values = f32(ref[...])
        center = values - jnp.mean(values, -1, keepdims=True)
        inverse = lax.rsqrt(jnp.mean(center * center, -1, keepdims=True) + epsilon_norm)
        normed[block * rows : (block + 1) * rows, :] = center * inverse
    for side, ref in enumerate((v_own, v_other)):
        offset = jnp.where(core == side, 0, half)
        part = normed[:, lanes(offset, half)]
        hidden[:, side * half : (side + 1) * half] = bf16(part * ref[0:1, :] + ref[1:2, :])
    for part in range(3):
        cut = lanes(part * width + core * half, half)
        total = jnp.dot(hidden[:, :half], w_own[:, cut], preferred_element_type=jnp.float32)
        total += jnp.dot(hidden[:, half:], w_other[:, cut], preferred_element_type=jnp.float32)
        if part != 1:
            row = 6 + part // 2
            total += v_own[row : row + 1, :]
        qkv[:, part * half : (part + 1) * half] = bf16(total)
    pair = 2 * HEAD_DIM
    low = lax.broadcasted_iota(jnp.int32, (rows, pair), 1) < HEAD_DIM
    for block in range(2):
        span = slice(block * rows, (block + 1) * rows)
        allowed = allowed_pairs(numbers, block, rows)
        for start in range(0, half, pair):
            query = qkv[span, start : start + pair]
            keys = qkv[span, half + start : half + start + pair]
            value = qkv[span, 2 * half + start : 2 * half + start + pair]
            zero = jnp.zeros_like(query)
            found = []
            for mine in (low, ~low):
                probs = head_probs(jnp.where(mine, query, zero), keys, allowed)
                found.append(jnp.dot(bf16(probs), value, preferred_element_type=jnp.float32))
            context[span, start : start + pair] = bf16(jnp.where(low, *found))


def attention_backward(place, numbers, grads, grads_other, w_out, qkv, grad_qkv, sums):
    rows = grads.shape[0]
    half = w_out.shape[0]
    pair = 2 * HEAD_DIM
    scale = HEAD_DIM ** (-0.5)
    low = lax.broadcasted_iota(jnp.int32, (rows, pair), 1) < HEAD_DIM
    sums[...] = jnp.zeros_like(sums)
    for block, ref in enumerate((grads, grads_other)):
        span = slice(block * rows, (block + 1) * rows)
        allowed = allowed_pairs(numbers, block, rows)
        grad_context = bf16(dot_nt(ref[...], w_out[...]))
        for start in range(0, half, pair):
            cut = slice(start, start + pair)
            query = qkv[span, start : start + pair]
            keys = qkv[span, half + start : half + start + pair]
            value = qkv[span, 2 * half + start : 2 * half + start + pair]
            above = grad_context[:, cut]
            zero = jnp.zeros_like(query)
            found = []
            for mine in (low, ~low):
                probs = head_probs(jnp.where(mine, query, zero), keys, allowed)
                grad_probs = dot_nt(jnp.where(mine, above, zero), value)
                delta = jnp.sum(probs * grad_probs, -1, keepdims=True)
                grad_scores = bf16(probs * (grad_probs - delta) * scale)
                found.append(
                    (
                        jnp.dot(grad_scores, keys, preferred_element_type=jnp.float32),
                        dot_tn(grad_scores, query),
                        dot_tn(bf16(probs), above),
                    )
                )
            for part, (first, second) in enumerate(zip(*found)):
                grad = jnp.where(low, first, second)
                grad_qkv[span, part * half + start : part * half + start + pair] = bf16(grad)
                if part != 1:
                    row = part // 2
                    sums[row : row + 1, cut] += jnp.sum(grad, 0, keepdims=True)


def store_blocks(place, first, second, keep, send, start):
    rows = keep.shape[1]
    flip, low_role = place[0], place[1]
    for i in range(first.shape[0] // rows):
        span = slice(i * rows, (i + 1) * rows)
        lower, upper = bf16(first[span]), bf16(second[span])
        where = (start // rows + i) ^ low_role
        keep[where] = jnp.where(flip == 0, lower, upper)
        send[where] = jnp.where(flip == 0, upper, lower)


def feed_piece(place, hidden, grad_out, w_up, up_bias, w_down, keep, send, act, grad_up, bias_sum):
    upper = jnp.dot(hidden[...], w_up[...], preferred_element_type=jnp.float32) + f32(up_bias[...])
    root = (2.0 / math.pi) ** 0.5
    square = upper * upper
    slope = jnp.tanh(root * (upper + 0.044715 * square * upper))
    act[...] = bf16(0.5 * upper * (1.0 + slope))
    derivative = 0.5 * (1.0 + slope) + 0.5 * upper * (1.0 - slope * slope) * root * (
        1.0 + 3.0 * 0.044715 * square
    )
    grad = dot_nt(grad_out[...], w_down[...]) * derivative
    bias_sum[...] = jnp.sum(grad, 0, keepdims=True)
    grad_up[...] = bf16(grad)
    size = act.shape[1]
    part = size // 2
    for start in range(0, size, part):
        cut = slice(start, start + part)
        store_blocks(
            place,
            dot_tn(act[:, cut], grad_out[...]),
            dot_tn(hidden[:, cut], grad_up[...]),
            keep,
            send,
            start,
        )


def middle_forward(
    place,
    numbers,
    context,
    context_other,
    w_out,
    w_out_other,
    tokens,
    tokens_other,
    v_own,
    v_other,
    cot,
    cot_other,
    w_up,
    up_bias,
    w_down,
    resid_out,
    hidden,
    grad_out,
    keep,
    send,
    act,
    grad_up,
    bias_sum,
    vectors,
):
    core = place[2]
    rows, width = tokens.shape
    half = width // 2
    last = numbers.shape[1] - 1
    vectors[:, lanes(core * half, half)] = v_own[...]
    vectors[:, lanes((1 - core) * half, half)] = v_other[...]
    for block, (token_ref, cot_ref) in enumerate(((tokens, cot), (tokens_other, cot_other))):
        span = slice(block * rows, (block + 1) * rows)
        out = jnp.dot(context[span, :], w_out[...], preferred_element_type=jnp.float32)
        out += jnp.dot(context_other[span, :], w_out_other[...], preferred_element_type=jnp.float32)
        resid = f32(token_ref[...]) + out + vectors[2:3, :]
        if block == 0:
            resid_out[...] = resid
        center = resid - jnp.mean(resid, -1, keepdims=True)
        inverse = lax.rsqrt(jnp.mean(center * center, -1, keepdims=True) + epsilon_norm)
        hidden[span, :] = bf16(center * inverse * vectors[3:4, :] + vectors[4:5, :])
        position = lax.broadcasted_iota(jnp.int32, (rows, width), 0)
        live = position < numbers[block, last]
        grad_out[span, :] = bf16(jnp.where(live, f32(cot_ref[...]), 0.0))
    feed_piece(
        place, hidden, grad_out, w_up, up_bias, w_down, keep, send, act, grad_up, bias_sum
    )


def attention_weights(
    place,
    hidden,
    grad_qkv,
    grad_qkv_other,
    context,
    grads,
    grads_other,
    w_own,
    w_other,
    keep,
    send,
    grad_own,
    grad_other,
):
    core = place[2]
    rows, width = grads.shape
    half = width // 2
    wide = 3 * half
    rows_block = keep.shape[1]
    left = hidden[:, :half]
    first = dot_tn(left, grad_qkv[...])
    second = dot_tn(hidden[:rows, :half], grad_qkv_other[rows:, :])
    second += dot_tn(hidden[rows:, :half], grad_qkv_other[:rows, :])
    third = dot_tn(context[:rows, :], grads[...]) + dot_tn(context[rows:, :], grads_other[...])
    flip, low_role = place[0], place[1]
    for i in range(half // rows_block):
        span = slice(i * rows_block, (i + 1) * rows_block)
        where = i ^ low_role
        for cut, lower, upper in (
            (slice(0, wide), first[span], second[span]),
            (slice(wide, wide + half), third[span, :half], third[span, half:]),
        ):
            lower, upper = bf16(lower), bf16(upper)
            keep[where, :, cut] = jnp.where(flip == 0, lower, upper)
            send[where, :, cut] = jnp.where(flip == 0, upper, lower)
    for side, ref in enumerate((w_own, w_other)):
        target = lanes(jnp.where(core == side, 0, half), half)
        total = jnp.zeros((2 * rows, half), jnp.float32)
        for part in range(3):
            cut = lanes(part * width + core * half, half)
            total += dot_nt(grad_qkv[:, part * half : (part + 1) * half], ref[:, cut])
        grad_own[:, target] = total[:rows]
        grad_other[:, target] = total[rows:]


def unpack_feed(own, other, place, before, hidden, piece):
    count, rows, width = own.shape
    kept = len(before)

    def kernel(place_ref, own_ref, other_ref, *refs):
        down_out, up_out = refs[kept:]
        mine, theirs = f32(own_ref[0]), f32(other_ref[0])
        down_out[...] = jnp.where(place_ref[0] == 0, mine, theirs)
        up_out[...] = jnp.where(place_ref[0] == 0, theirs, mine)

    block = pl.BlockSpec((1, rows, width), lambda i, place_ref: (i ^ place_ref[1], 0, 0))
    return pl.pallas_call(
        kernel,
        out_shape=[
            jax.ShapeDtypeStruct((hidden, width), jnp.float32),
            jax.ShapeDtypeStruct((width, hidden), jnp.float32),
        ],
        grid_spec=pltpu.PrefetchScalarGridSpec(
            num_scalar_prefetch=1,
            grid=(count,),
            in_specs=[block, block] + [pl.BlockSpec(memory_space=pl.ANY)] * kept,
            out_specs=[
                pl.BlockSpec((rows, width), lambda i, place_ref: (piece * count + i, 0)),
                pl.BlockSpec((rows, width), lambda i, place_ref: (i, piece)),
            ],
        ),
        input_output_aliases={3: 0, 4: 1} if kept else {},
    )(place, own, other, *before)


def unpack_attention(own, other, place):
    count, rows, wide = own.shape
    half = wide // 4

    def kernel(place_ref, own_ref, other_ref, qkv_out, out_out):
        mine, theirs = f32(own_ref[0]), f32(other_ref[0])
        first = jnp.where(place_ref[0] == 0, mine, theirs)
        second = jnp.where(place_ref[0] == 0, theirs, mine)
        core = place_ref[2]
        for part in range(3):
            cut = slice(part * half, (part + 1) * half)
            base = part * 2 * half
            qkv_out[:, lanes(base + core * half, half)] = first[:, cut]
            qkv_out[:, lanes(base + (1 - core) * half, half)] = second[:, cut]
        out_out[:, :half] = first[:, 3 * half :]
        out_out[:, half:] = second[:, 3 * half :]

    block = pl.BlockSpec((1, rows, wide), lambda i, place_ref: (i ^ place_ref[1], 0, 0))
    return pl.pallas_call(
        kernel,
        out_shape=[
            jax.ShapeDtypeStruct((count * rows, 6 * half), jnp.float32),
            jax.ShapeDtypeStruct((count * rows, 2 * half), jnp.float32),
        ],
        grid_spec=pltpu.PrefetchScalarGridSpec(
            num_scalar_prefetch=1,
            grid=(count,),
            in_specs=[block, block],
            out_specs=[
                pl.BlockSpec((rows, 6 * half), lambda i, place_ref: (i, 0)),
                pl.BlockSpec((rows, 2 * half), lambda i, place_ref: (i, 0)),
            ],
        ),
    )(place, own, other)


def pair_local(
    tokens_in,
    cotangent,
    seq_lengths,
    live_counts,
    ln1_gain,
    ln1_shift,
    w_qkv,
    q_bias,
    v_bias,
    w_out,
    out_bias,
    ln2_gain,
    ln2_shift,
    w_up,
    up_bias,
    w_down,
    down_bias,
    reps,
):
    core, rep = lax.axis_index("shard"), lax.axis_index("rep")
    first = core == 0

    def swap(array):
        return exchange(array, "shard", 1, 2)

    def natural(own, other):
        return jnp.concatenate([jnp.where(first, own, other), jnp.where(first, other, own)], 1)

    order = rep_order(reps)
    role = 0
    for distances in order:
        distance = jnp.where(first, *distances)
        role = 2 * role + (rep // distance) % 2
    top = reps // 2
    place = jnp.stack([role // top, role % top, core]).astype(jnp.int32)

    rows, width = tokens_in.shape
    half = width // 2
    hidden = w_up.shape[1]
    both = 2 * rows
    wide = 3 * half
    b, f = jnp.bfloat16, jnp.float32
    w_other = swap(w_qkv)
    tokens_other = swap(tokens_in)
    small = (ln1_gain, ln1_shift, out_bias, ln2_gain, ln2_shift, down_bias, q_bias, v_bias)
    row = lax.broadcasted_iota(jnp.int32, (len(small), half), 0)
    v_own = sum(jnp.where(row == i, f32(v)[None], 0.0) for i, v in enumerate(small))
    v_other = swap(v_own)
    numbers = jnp.concatenate([seq_lengths, live_counts[:, None]], 1)
    numbers = jnp.concatenate([numbers, swap(numbers)], 0)
    w_out_other = swap(w_out)
    cot_other = swap(cotangent)
    hidden_one, qkv, context = call(
        attention_forward,
        [((both, width), b), ((both, wide), b), ((both, half), b)],
        (place, numbers, tokens_in, tokens_other, w_qkv, w_other, v_own, v_other),
        2,
        [pltpu.VMEM((both, width), f)],
        2 * both * width * wide,
    )
    context_other = swap(jnp.concatenate([context[rows:], context[:rows]], 0))
    pieces = hidden // width
    biases = up_bias[None]
    block = 2 * width // reps
    packed = ((top, block, width), b)
    piece_outs = [packed, packed, ((both, width), b), ((both, width), b), ((1, width), f)]
    feeds = []
    flops = 8 * both * width * width
    for i in range(pieces):
        cut = slice(i * width, (i + 1) * width)
        weights = (w_up[:, cut], biases[:, cut], w_down[cut])
        if i == 0:
            resid, hidden_two, grad_out_b, *outs = call(
                middle_forward,
                [((rows, width), f), ((both, width), b), ((both, width), b)] + piece_outs,
                (
                    place,
                    numbers,
                    context,
                    context_other,
                    w_out,
                    w_out_other,
                    tokens_in,
                    tokens_other,
                    v_own,
                    v_other,
                    cotangent,
                    cot_other,
                )
                + weights,
                2,
                [pltpu.VMEM((8, width), f)],
                flops,
            )
        else:
            outs = call(
                feed_piece, piece_outs, (place, hidden_two, grad_out_b) + weights, 1, (), flops
            )
        feeds.append(outs)
    vectors = natural(v_own, v_other)
    gain_one, gain_two, bias_down = vectors[0], vectors[3], vectors[5]
    acts = [outs[2] for outs in feeds]
    grad_ups = [outs[3] for outs in feeds]

    def back(span):
        return sum(
            matmul(g[span], w_up[:, i * width : (i + 1) * width].T) for i, g in enumerate(grad_ups)
        )

    def ahead(span):
        return sum(
            matmul(a[span], w_down[i * width : (i + 1) * width]) for i, a in enumerate(acts)
        )

    mine, theirs = slice(0, rows), slice(rows, both)
    live_col = f32(jnp.arange(rows, dtype=jnp.int32) < live_counts[0])[:, None]
    grad_hidden_two = back(mine) + swap(back(theirs))
    grad_out = f32(cotangent) * live_col
    _, normed_two, inverse_two = norm_forward(resid, 1.0, 0.0)
    grad_resid_norm, grad_gain_two, grad_shift_two = norm_backward(
        grad_hidden_two, normed_two, inverse_two, gain_two
    )
    grad_resid = grad_out + grad_resid_norm
    grad_resid_b = bf16(grad_resid)
    grad_resid_other = swap(grad_resid_b)
    grad_qkv, sums = call(
        attention_backward,
        [((both, wide), b), ((8, half), f)],
        (place, numbers, grad_resid_b, grad_resid_other, w_out, qkv),
        2,
        (),
        4 * both * width * half,
    )
    grad_qkv_other = swap(grad_qkv)
    packed = ((top, 2 * half // reps, wide + half), b)
    keep, send, grad_one, grad_one_other = call(
        attention_weights,
        [packed, packed, ((rows, width), f), ((rows, width), f)],
        (
            place,
            hidden_one,
            grad_qkv,
            grad_qkv_other,
            context,
            grad_resid_b,
            grad_resid_other,
            w_qkv,
            w_other,
        ),
        1,
        (),
        6 * both * width * wide // 2,
    )
    grad_hidden_one = grad_one + swap(grad_one_other)
    _, normed_one, inverse_one = norm_forward(f32(tokens_in), 1.0, 0.0)
    grad_in_norm, grad_gain_one, grad_shift_one = norm_backward(
        grad_hidden_one, normed_one, inverse_one, gain_one
    )
    grad_in = bf16(grad_resid + grad_in_norm)
    result = bf16((resid + ahead(mine) + swap(ahead(theirs)) + bias_down) * live_col)
    sums_feed = ()
    for i, outs in enumerate(feeds):
        halves = rep_sum(outs[0], outs[1], order, reps)
        sums_feed = unpack_feed(*halves, place, sums_feed, hidden, i)
    grad_wdown, grad_wup = sums_feed
    grad_wqkv, grad_wout = unpack_attention(*rep_sum(keep, send, order, reps), place)
    wide_sums = (
        grad_gain_one,
        grad_shift_one,
        jnp.sum(grad_resid, 0),
        grad_gain_two,
        grad_shift_two,
        jnp.sum(grad_out, 0),
    )
    row = lax.broadcasted_iota(jnp.int32, (len(wide_sums), width), 0)
    table = sum(jnp.where(row == i, v[None], 0.0) for i, v in enumerate(wide_sums))
    own = jnp.where(first, table[:, :half], table[:, half:])
    other = jnp.where(first, table[:, half:], table[:, :half])
    up_sums = jnp.concatenate([outs[4].reshape(-1, half) for outs in feeds], 0)
    pack = small_sum(jnp.concatenate([own + swap(other), sums[:2], up_sums], 0), reps)
    return (
        result,
        grad_in,
        pack[0],
        pack[1],
        grad_wqkv,
        pack[6],
        pack[7],
        grad_wout,
        pack[2],
        pack[3],
        pack[4],
        grad_wup,
        pack[8:].reshape(-1),
        grad_wdown,
        pack[5],
    )


def rep_order(reps):
    line = [(1 << i, 1 << i) for i in range(2, reps.bit_length() - 1)]
    return [(1, 2), (2, 1)] + line


def pair_fits(mesh):
    reps = mesh.shape["rep"]
    return mesh.shape["shard"] == 2 and 4 <= reps <= 16 and reps & (reps - 1) == 0


def solution(mesh):
    local = plain_local
    if pair_fits(mesh):
        local = functools.partial(pair_local, reps=mesh.shape["rep"])
    return jax.shard_map(
        local,
        mesh=mesh,
        in_specs=(
            P(("rep", "shard"), None),
            P(("rep", "shard"), None),
            P(("rep", "shard"), None),
            P(("rep", "shard")),
            P("shard"),
            P("shard"),
            P("shard", None),
            P("shard"),
            P("shard"),
            P("shard", None),
            P("shard"),
            P("shard"),
            P("shard"),
            P(None, "shard"),
            P("shard"),
            P("shard", None),
            P("shard"),
        ),
        out_specs=(
            P(("rep", "shard"), None),
            P(("rep", "shard"), None),
            P("shard"),
            P("shard"),
            P("shard", None),
            P("shard"),
            P("shard"),
            P("shard", None),
            P("shard"),
            P("shard"),
            P("shard"),
            P(None, "shard"),
            P("shard"),
            P("shard", None),
            P("shard"),
        ),
        check_vma=False,
    )
```
